32 devices in a mesh: grid: 8 (over z, core), vec: 4 (over y, x).
Axes of the slice: x: 2, y: 2, z: 4, core: 2. Of those that a mesh axis runs over, the one named last changes fastest.
Arguments:
- orbitals: bfloat16 [884736, 512], P(('grid', 'vec')), may hold values from -1.296875 to 1.296875
- inverse_panel: bfloat16 [2048, 32], replicated, may hold values from -0.125 to 0.125
- points: int32 [2048], replicated, may hold values from 0 to 884735, as said below
Outputs:
- projected: float32 [2048, 32], P(('grid', 'vec'))
The draws below stay inside these ranges and needn't reach their ends.
Inputs may be any that keep to these rules, and one draw needn't show every extreme that they name: `points`: distinct cell indices.
All inputs are finite; a program needn't handle non-finite values.
Results may differ from the reference program's by a relative error of at most 0.005.
Values may be sent and summed in bfloat16 or wider, within the bound.
A program may use at most 256 MiB of HBM per device.

```python
import math
import jax
import jax.numpy as jnp
from jax import lax

NG = 96
NORB = 512
NPTS = 2048
COLS = 32


def draw_points(key, part):
    return jax.random.permutation(key, NG ** 3)[:NPTS].astype(jnp.int32)


def block_scale(stream_key, shape, cuts, least, high):
    level = 1.0
    for position, parts in cuts:
        draws = jax.random.uniform(jax.random.fold_in(jax.random.fold_in(stream_key, 6), position), (parts,), jnp.float32, least / len(cuts), high / len(cuts))
        level = level * jnp.repeat(jnp.exp(draws), shape[position] // parts).reshape((-1,) + (1,) * (len(shape) - 1 - position))
    return level


def normal_values(stream_key, dims, width, limit, shards=(), held_as=jnp.bfloat16):
    values = jax.random.normal(stream_key, dims, jnp.float32) * width
    if len(shards) > 0:
        values = block_scale(stream_key, dims, shards, -0.22, 0.18) * values
    return jnp.clip(values, min=-limit, max=limit).astype(held_as)


def setup_inputs(seed: int = 0) -> dict:
    seeds = jax.random.split(jax.random.key(seed), 4)
    return {
        "orbitals": normal_values(seeds[0], (NG**3, NORB), 0.21, 1.296875, ((0, 32),)),
        "inverse_panel": normal_values(seeds[1], (NPTS, COLS), NPTS ** -0.5, 0.125),
        "points": draw_points(jax.random.fold_in(seeds[3], 71), 0),
    }


SCREEN = 2.25

def wave_tables(count):
    index = lax.iota(jnp.int32, count)
    phase = index[:, None] * index[None, :] % count
    angle = phase.astype(jnp.float32) * (2.0 * math.pi / count)
    return (jnp.cos(angle).astype(jnp.bfloat16), jnp.sin(angle).astype(jnp.bfloat16))

def wavenumber(index, count):
    return jnp.where(index < count // 2, index, index - count).astype(jnp.float32)

def screened(wave_x, wave_y, wave_z):
    squared = wave_x[:, None, None] * wave_x[:, None, None] + wave_y[None, :, None] * wave_y[None, :, None] + wave_z[None, None, :] * wave_z[None, None, :]
    factor = NG / (2.0 * math.pi) * (NG / (2.0 * math.pi))
    return jnp.where(squared > 0.5, factor / (squared + SCREEN), jnp.float32(0.0))

def contract(data, table, form):
    return jnp.einsum(form, data.astype(jnp.float32), table.astype(jnp.float32))

def poisson(column, cos_tab, sin_tab, kernel):
    bf = jnp.bfloat16
    z_re = contract(column, cos_tab, 'xyz,zk->xyk').astype(bf)
    z_im = (-contract(column, sin_tab, 'xyz,zk->xyk')).astype(bf)
    y_re = (contract(z_re, cos_tab, 'xyz,yk->xkz') + contract(z_im, sin_tab, 'xyz,yk->xkz')).astype(bf)
    y_im = (contract(z_im, cos_tab, 'xyz,yk->xkz') - contract(z_re, sin_tab, 'xyz,yk->xkz')).astype(bf)
    x_re = contract(y_re, cos_tab, 'xyz,xk->kyz') + contract(y_im, sin_tab, 'xyz,xk->kyz')
    x_im = contract(y_im, cos_tab, 'xyz,xk->kyz') - contract(y_re, sin_tab, 'xyz,xk->kyz')
    q_re = (x_re * kernel).astype(bf)
    q_im = (x_im * kernel).astype(bf)
    i_re = (contract(q_re, cos_tab, 'xyz,xk->kyz') - contract(q_im, sin_tab, 'xyz,xk->kyz')).astype(bf)
    i_im = (contract(q_im, cos_tab, 'xyz,xk->kyz') + contract(q_re, sin_tab, 'xyz,xk->kyz')).astype(bf)
    h_re = (contract(i_re, cos_tab, 'xyz,yk->xkz') - contract(i_im, sin_tab, 'xyz,yk->xkz')).astype(bf)
    h_im = (contract(i_im, cos_tab, 'xyz,yk->xkz') + contract(i_re, sin_tab, 'xyz,yk->xkz')).astype(bf)
    final = contract(h_re, cos_tab, 'xyz,zk->xyk') - contract(h_im, sin_tab, 'xyz,zk->xyk')
    return (final / float(NG ** 3)).astype(bf)

def reference(orbitals, inverse_panel, points):
    point_rows = orbitals[points]
    blocks = orbitals.reshape(NG, NG * NG, NORB)

    def make_pair(block):
        correlation = jnp.dot(block, point_rows.T, preferred_element_type=jnp.float32)
        return (correlation * correlation).astype(jnp.bfloat16)

    def fit_block(block):
        return jnp.dot(make_pair(block), inverse_panel, preferred_element_type=jnp.float32).astype(jnp.bfloat16)
    fitted = lax.map(fit_block, blocks)
    field = jnp.moveaxis(fitted.reshape(NG, NG, NG, COLS), 3, 0)
    cos_tab, sin_tab = wave_tables(NG)
    waves = wavenumber(lax.iota(jnp.int32, NG), NG)
    kernel = screened(waves, waves, waves)
    potential = lax.map(lambda column: poisson(column, cos_tab, sin_tab, kernel), field)
    pot_blocks = jnp.moveaxis(potential.reshape(COLS, NG, NG * NG), 1, 0)

    def accumulate(total, pieces):
        block, pot_block = pieces
        pair = make_pair(block)
        term = lax.dot_general(pair, pot_block, (((0,), (1,)), ((), ())), preferred_element_type=jnp.float32)
        return (total + term, None)
    total, _ = lax.scan(accumulate, jnp.zeros((NPTS, COLS), jnp.float32), (blocks, pot_blocks))
    return total * jnp.float32(1.0 / math.sqrt(float(NG ** 3)))
```

```python
import math

import jax
import jax.numpy as jnp
from jax import lax
from jax.sharding import PartitionSpec as P

NG = 96


SCREEN = 2.25


def wave_tables(count):
    index = lax.iota(jnp.int32, count)
    phase = index[:, None] * index[None, :] % count
    angle = phase.astype(jnp.float32) * (2.0 * math.pi / count)
    return (jnp.cos(angle).astype(jnp.bfloat16), jnp.sin(angle).astype(jnp.bfloat16))


def wavenumber(index, count):
    return jnp.where(index < count // 2, index, index - count).astype(jnp.float32)


def screened(wave_x, wave_y, wave_z):
    squared = (
        wave_x[:, None, None] * wave_x[:, None, None]
        + wave_y[None, :, None] * wave_y[None, :, None]
        + wave_z[None, None, :] * wave_z[None, None, :]
    )
    factor = NG / (2.0 * math.pi) * (NG / (2.0 * math.pi))
    return jnp.where(squared > 0.5, factor / (squared + SCREEN), jnp.float32(0.0))


def mult(data, table, form):
    return jnp.einsum(form, data, table, preferred_element_type=jnp.float32)


def transform(re, im, cos_tab, sin_tab, form, sign):
    out_re = mult(re, cos_tab, form) + sign * mult(im, sin_tab, form)
    out_im = mult(im, cos_tab, form) - sign * mult(re, sin_tab, form)
    return out_re, out_im


def solve_columns(fit_cols):
    bf = jnp.bfloat16
    axes = ("grid", "vec")
    flat = lax.all_to_all(fit_cols, axes, split_axis=0, concat_axis=1, tiled=True)
    field = flat.reshape(flat.shape[0], NG, NG, NG)
    cos_tab, sin_tab = wave_tables(NG)
    waves = wavenumber(lax.iota(jnp.int32, NG), NG)
    kernel = screened(waves, waves, waves)[None]
    a_re = mult(field, cos_tab, "vxyz,zk->vxyk").astype(bf)
    a_im = (-mult(field, sin_tab, "vxyz,zk->vxyk")).astype(bf)
    b_re, b_im = transform(a_re, a_im, cos_tab, sin_tab, "vxyz,yk->vxkz", 1.0)
    b_re, b_im = b_re.astype(bf), b_im.astype(bf)
    h_re, h_im = transform(b_re, b_im, cos_tab, sin_tab, "vxyz,xk->vkyz", 1.0)
    q_re, q_im = (h_re * kernel).astype(bf), (h_im * kernel).astype(bf)
    g_re, g_im = transform(q_re, q_im, cos_tab, sin_tab, "vxyz,xk->vkyz", -1.0)
    g_re, g_im = g_re.astype(bf), g_im.astype(bf)
    p_re, p_im = transform(g_re, g_im, cos_tab, sin_tab, "vxyz,yk->vxkz", -1.0)
    p_re, p_im = p_re.astype(bf), p_im.astype(bf)
    final = mult(p_re, cos_tab, "vxyz,zk->vxyk") - mult(p_im, sin_tab, "vxyz,zk->vxyk")
    potential = (final / float(NG**3)).astype(bf).reshape(flat.shape)
    return lax.all_to_all(potential, axes, split_axis=1, concat_axis=0, tiled=True)


def project(pair, pot_rows):
    scale = 1.0 / math.sqrt(float(NG**3))
    term = lax.dot_general(
        pair, pot_rows, (((0,), (1,)), ((), ())), preferred_element_type=jnp.float32
    )
    return lax.psum_scatter(
        term * jnp.float32(scale), ("grid", "vec"), scatter_dimension=0, tiled=True
    )


def shards(orbitals, inverse_panel, points):
    bf = jnp.bfloat16
    row_count = orbitals.shape[0]
    grid_count = lax.axis_size("grid")
    vec_count = lax.axis_size("vec")
    npoints = points.shape[0]
    offset = (lax.axis_index("grid") * vec_count + lax.axis_index("vec")) * row_count
    local_pos = points - offset
    inside = (local_pos >= 0) & (local_pos < row_count)
    picked = jnp.take(orbitals, jnp.clip(local_pos, 0, row_count - 1), axis=0)
    picked = jnp.where(inside[:, None], picked, jnp.zeros_like(picked))
    point_rows = lax.psum(picked, ("grid", "vec"))

    def pair_block(block):
        correlation = lax.dot_general(
            block, point_rows, (((1,), (1,)), ((), ())), preferred_element_type=jnp.float32
        )
        return (correlation * correlation).astype(bf)

    pair = lax.map(pair_block, orbitals.reshape(4, row_count // 4, orbitals.shape[1])).reshape(
        row_count, npoints
    )
    fit_cols = lax.dot_general(
        inverse_panel, pair, (((0,), (1,)), ((), ())), preferred_element_type=jnp.float32
    ).astype(bf)
    if inverse_panel.shape[1] % (grid_count * vec_count) == 0:
        return project(pair, solve_columns(fit_cols))
    slab = lax.all_to_all(fit_cols, "vec", split_axis=0, concat_axis=1, tiled=True)
    col_local = slab.shape[0]
    planes = NG // grid_count
    field = slab.reshape(col_local, planes, NG, NG)
    cos_tab, sin_tab = wave_tables(NG)
    z_re = mult(field, cos_tab, "vxyz,zk->vxyk").astype(bf)
    z_im = (-mult(field, sin_tab, "vxyz,zk->vxyk")).astype(bf)
    y_re = (mult(z_re, cos_tab, "vxyz,yk->vxkz") + mult(z_im, sin_tab, "vxyz,yk->vxkz")).astype(bf)
    y_im = (mult(z_im, cos_tab, "vxyz,yk->vxkz") - mult(z_re, sin_tab, "vxyz,yk->vxkz")).astype(bf)
    stacked = jnp.stack([y_re, y_im])
    waves = wavenumber(lax.iota(jnp.int32, NG), NG)
    y_waves = wavenumber(lax.axis_index("grid") * planes + lax.iota(jnp.int32, planes), NG)
    kernel = screened(waves, y_waves, waves)[None]
    piece = lax.all_to_all(stacked, "grid", split_axis=3, concat_axis=2, tiled=True)
    p_re = piece[0]
    p_im = piece[1]
    x_re = mult(p_re, cos_tab, "vxyz,xk->vkyz") + mult(p_im, sin_tab, "vxyz,xk->vkyz")
    x_im = mult(p_im, cos_tab, "vxyz,xk->vkyz") - mult(p_re, sin_tab, "vxyz,xk->vkyz")
    q_re = (x_re * kernel).astype(bf)
    q_im = (x_im * kernel).astype(bf)
    i_re = (mult(q_re, cos_tab, "vxyz,xk->vkyz") - mult(q_im, sin_tab, "vxyz,xk->vkyz")).astype(bf)
    i_im = (mult(q_im, cos_tab, "vxyz,xk->vkyz") + mult(q_re, sin_tab, "vxyz,xk->vkyz")).astype(bf)
    spectrum = lax.all_to_all(
        jnp.stack([i_re, i_im]), "grid", split_axis=2, concat_axis=3, tiled=True
    )
    s_re = spectrum[0]
    s_im = spectrum[1]
    h_re = (mult(s_re, cos_tab, "vxyz,yk->vxkz") - mult(s_im, sin_tab, "vxyz,yk->vxkz")).astype(bf)
    h_im = (mult(s_im, cos_tab, "vxyz,yk->vxkz") + mult(s_re, sin_tab, "vxyz,yk->vxkz")).astype(bf)
    final = mult(h_re, cos_tab, "vxyz,zk->vxyk") - mult(h_im, sin_tab, "vxyz,zk->vxyk")
    potential = (final / float(NG**3)).astype(bf).reshape(col_local, planes * NG * NG)
    pot_rows = lax.all_to_all(potential, "vec", split_axis=1, concat_axis=0, tiled=True)
    return project(pair, pot_rows)


def solution(mesh):
    in_specs = (P(("grid", "vec"), None), P(), P())
    out_specs = P(("grid", "vec"), None)
    return jax.shard_map(shards, mesh=mesh, in_specs=in_specs, out_specs=out_specs, check_vma=False)
```

```python
import math

import jax
import jax.numpy as jnp
from jax import lax
from jax.experimental import pallas as pl
from jax.experimental.pallas import tpu as pltpu
from jax.sharding import PartitionSpec as P

NG = 96


SCREEN = 2.25


def wave_tables(count):
    index = lax.iota(jnp.int32, count)
    phase = index[:, None] * index[None, :] % count
    angle = phase.astype(jnp.float32) * (2.0 * math.pi / count)
    return (jnp.cos(angle).astype(jnp.bfloat16), jnp.sin(angle).astype(jnp.bfloat16))


def wavenumber(index, count):
    return jnp.where(index < count // 2, index, index - count).astype(jnp.float32)


def screened(wave_x, wave_y, wave_z):
    squared = (
        wave_x[:, None, None] * wave_x[:, None, None]
        + wave_y[None, :, None] * wave_y[None, :, None]
        + wave_z[None, None, :] * wave_z[None, None, :]
    )
    factor = NG / (2.0 * math.pi) * (NG / (2.0 * math.pi))
    return jnp.where(squared > 0.5, factor / (squared + SCREEN), jnp.float32(0.0))


def mult(data, table, form):
    return jnp.einsum(form, data, table, preferred_element_type=jnp.float32)


LANES = 128


def exchange_kernel(total, x_ref, o_ref, held, send_sem, recv_sem, own_sem):
    vec_count = lax.axis_size("vec")
    count = lax.axis_size("grid") * vec_count
    me = lax.axis_index("grid") * vec_count + lax.axis_index("vec")
    land = held if total else o_ref

    def place(index):
        return (index // vec_count, lax.rem(index, vec_count))

    barrier = pltpu.get_barrier_semaphore()

    def greet(step, carry):
        pl.semaphore_signal(
            barrier,
            inc=1,
            device_id=place(lax.rem(me + step, count)),
            device_id_type=pl.DeviceIdType.MESH,
        )
        return carry

    lax.fori_loop(1, count, greet, 0)
    own = pltpu.make_async_copy(x_ref.at[me], land.at[me], own_sem)
    own.start()
    pl.semaphore_wait(barrier, count - 1)

    def copy(step, source, slot):
        peer = lax.rem(me + step, count)
        return pltpu.make_async_remote_copy(
            src_ref=x_ref.at[source],
            dst_ref=land.at[slot],
            send_sem=send_sem.at[step],
            recv_sem=recv_sem.at[step],
            device_id=place(peer),
            device_id_type=pl.DeviceIdType.MESH,
        )

    def send(step, carry):
        copy(step, lax.rem(me + step, count), me).start()
        return carry

    lax.fori_loop(1, count, send, 0)
    own.wait()

    def receive(step, carry):
        source = lax.rem(me + count - step, count)
        copy(step, source, source).wait_recv()
        return carry

    lax.fori_loop(1, count, receive, 0)
    if total:
        o_ref[...] = jnp.sum(held[...], axis=0)

    def drain(step, carry):
        copy(step, lax.rem(me + step, count), me).wait_send()
        return carry

    lax.fori_loop(1, count, drain, 0)


def exchange(blocks, ident, total=False):
    count, rows, lanes = blocks.shape
    shape = (rows, lanes) if total else blocks.shape
    held_shape = blocks.shape if total else (1, 8, LANES)

    def body(*refs):
        exchange_kernel(total, *refs)

    return pl.pallas_call(
        body,
        out_shape=jax.ShapeDtypeStruct(shape, blocks.dtype),
        in_specs=[pl.BlockSpec(memory_space=pltpu.VMEM)],
        out_specs=pl.BlockSpec(memory_space=pltpu.VMEM),
        scratch_shapes=[
            pltpu.VMEM(held_shape, blocks.dtype),
            pltpu.SemaphoreType.DMA((count,)),
            pltpu.SemaphoreType.DMA((count,)),
            pltpu.SemaphoreType.DMA(()),
        ],
        compiler_params=pltpu.CompilerParams(
            collective_id=ident, has_side_effects=True, vmem_limit_bytes=32 << 20
        ),
        name="exchange_total" if total else "exchange_blocks",
    )(blocks)


def transform(re, im, cos_tab, sin_tab, form, sign):
    out_re = mult(re, cos_tab, form) + sign * mult(im, sin_tab, form)
    out_im = mult(im, cos_tab, form) - sign * mult(re, sin_tab, form)
    return out_re, out_im


def solve_columns(fit_cols):
    bf = jnp.bfloat16
    count = fit_cols.shape[0]
    rows = fit_cols.shape[1]
    flat = exchange(fit_cols.reshape(count, rows // LANES, LANES), 1)
    field = flat.reshape(1, NG, NG, NG)
    cos_tab, sin_tab = wave_tables(NG)
    waves = wavenumber(lax.iota(jnp.int32, NG), NG)
    kernel = screened(waves, waves, waves)[None]
    a_re = mult(field, cos_tab, "vxyz,zk->vxyk").astype(bf)
    a_im = (-mult(field, sin_tab, "vxyz,zk->vxyk")).astype(bf)
    b_re, b_im = transform(a_re, a_im, cos_tab, sin_tab, "vxyz,yk->vxkz", 1.0)
    b_re, b_im = b_re.astype(bf), b_im.astype(bf)
    h_re, h_im = transform(b_re, b_im, cos_tab, sin_tab, "vxyz,xk->vkyz", 1.0)
    q_re, q_im = (h_re * kernel).astype(bf), (h_im * kernel).astype(bf)
    g_re, g_im = transform(q_re, q_im, cos_tab, sin_tab, "vxyz,xk->vkyz", -1.0)
    g_re, g_im = g_re.astype(bf), g_im.astype(bf)
    p_re, p_im = transform(g_re, g_im, cos_tab, sin_tab, "vxyz,yk->vxkz", -1.0)
    p_re, p_im = p_re.astype(bf), p_im.astype(bf)
    final = mult(p_re, cos_tab, "vxyz,zk->vxyk") - mult(p_im, sin_tab, "vxyz,zk->vxyk")
    potential = (final / float(NG**3)).astype(bf).reshape(flat.shape)
    return exchange(potential, 2).reshape(count, rows)


def project(pair, pot_rows):
    scale = 1.0 / math.sqrt(float(NG**3))
    term = lax.dot_general(
        pair, pot_rows, (((0,), (1,)), ((), ())), preferred_element_type=jnp.float32
    )
    term = term * jnp.float32(scale)
    npoints, cols = term.shape
    count = lax.axis_size("grid") * lax.axis_size("vec")
    share = npoints // count
    if share * cols % LANES == 0:
        blocks = term.reshape(count, share * cols // LANES, LANES)
        return exchange(blocks, 3, True).reshape(share, cols)
    partial_block = lax.psum_scatter(term, "grid", scatter_dimension=0, tiled=True)
    return lax.psum_scatter(partial_block, "vec", scatter_dimension=0, tiled=True)


def shards(orbitals, inverse_panel, points):
    bf = jnp.bfloat16
    row_count = orbitals.shape[0]
    grid_count = lax.axis_size("grid")
    vec_count = lax.axis_size("vec")
    npoints = points.shape[0]
    offset = (lax.axis_index("grid") * vec_count + lax.axis_index("vec")) * row_count
    local_pos = points - offset
    inside = (local_pos >= 0) & (local_pos < row_count)
    picked = jnp.take(orbitals, jnp.clip(local_pos, 0, row_count - 1), axis=0)
    picked = jnp.where(inside[:, None], picked, jnp.zeros_like(picked)).astype(jnp.float32)
    summed_rows = lax.psum(picked, ("grid", "vec"))
    point_rows = summed_rows.astype(bf)

    def pair_block(block):
        correlation = lax.dot_general(
            block, point_rows, (((1,), (1,)), ((), ())), preferred_element_type=jnp.float32
        )
        return (correlation * correlation).astype(bf)

    pair = lax.map(pair_block, orbitals.reshape(4, row_count // 4, orbitals.shape[1])).reshape(
        row_count, npoints
    )
    fit_cols = lax.dot_general(
        inverse_panel, pair, (((0,), (1,)), ((), ())), preferred_element_type=jnp.float32
    ).astype(bf)
    if inverse_panel.shape[1] == grid_count * vec_count and row_count % LANES == 0:
        return project(pair, solve_columns(fit_cols))
    slab = lax.all_to_all(fit_cols, "vec", split_axis=0, concat_axis=1, tiled=True)
    col_local = slab.shape[0]
    planes = NG // grid_count
    field = slab.reshape(col_local, planes, NG, NG)
    cos_tab, sin_tab = wave_tables(NG)
    z_re = mult(field, cos_tab, "vxyz,zk->vxyk").astype(bf)
    z_im = (-mult(field, sin_tab, "vxyz,zk->vxyk")).astype(bf)
    y_re = (mult(z_re, cos_tab, "vxyz,yk->vxkz") + mult(z_im, sin_tab, "vxyz,yk->vxkz")).astype(bf)
    y_im = (mult(z_im, cos_tab, "vxyz,yk->vxkz") - mult(z_re, sin_tab, "vxyz,yk->vxkz")).astype(bf)
    stacked = jnp.stack([y_re, y_im])
    waves = wavenumber(lax.iota(jnp.int32, NG), NG)
    y_waves = wavenumber(lax.axis_index("grid") * planes + lax.iota(jnp.int32, planes), NG)
    kernel = screened(waves, y_waves, waves)[None]
    piece = lax.all_to_all(stacked, "grid", split_axis=3, concat_axis=2, tiled=True)
    p_re = piece[0]
    p_im = piece[1]
    x_re = mult(p_re, cos_tab, "vxyz,xk->vkyz") + mult(p_im, sin_tab, "vxyz,xk->vkyz")
    x_im = mult(p_im, cos_tab, "vxyz,xk->vkyz") - mult(p_re, sin_tab, "vxyz,xk->vkyz")
    q_re = (x_re * kernel).astype(bf)
    q_im = (x_im * kernel).astype(bf)
    i_re = (mult(q_re, cos_tab, "vxyz,xk->vkyz") - mult(q_im, sin_tab, "vxyz,xk->vkyz")).astype(bf)
    i_im = (mult(q_im, cos_tab, "vxyz,xk->vkyz") + mult(q_re, sin_tab, "vxyz,xk->vkyz")).astype(bf)
    spectrum = lax.all_to_all(
        jnp.stack([i_re, i_im]), "grid", split_axis=2, concat_axis=3, tiled=True
    )
    s_re = spectrum[0]
    s_im = spectrum[1]
    h_re = (mult(s_re, cos_tab, "vxyz,yk->vxkz") - mult(s_im, sin_tab, "vxyz,yk->vxkz")).astype(bf)
    h_im = (mult(s_im, cos_tab, "vxyz,yk->vxkz") + mult(s_re, sin_tab, "vxyz,yk->vxkz")).astype(bf)
    final = mult(h_re, cos_tab, "vxyz,zk->vxyk") - mult(h_im, sin_tab, "vxyz,zk->vxyk")
    potential = (final / float(NG**3)).astype(bf).reshape(col_local, planes * NG * NG)
    pot_rows = lax.all_to_all(potential, "vec", split_axis=1, concat_axis=0, tiled=True)
    return project(pair, pot_rows)


def solution(mesh):
    in_specs = (P(("grid", "vec"), None), P(), P())
    out_specs = P(("grid", "vec"), None)
    return jax.shard_map(shards, mesh=mesh, in_specs=in_specs, out_specs=out_specs, check_vma=False)
```

```python
import math

import jax
import jax.numpy as jnp
from jax import lax
from jax.experimental import pallas as pl
from jax.experimental.pallas import tpu as pltpu
from jax.sharding import PartitionSpec as P

NG = 96


SCREEN = 2.25


def wave_tables(count):
    index = lax.iota(jnp.int32, count)
    phase = index[:, None] * index[None, :] % count
    angle = phase.astype(jnp.float32) * (2.0 * math.pi / count)
    return (jnp.cos(angle).astype(jnp.bfloat16), jnp.sin(angle).astype(jnp.bfloat16))


def wavenumber(index, count):
    return jnp.where(index < count // 2, index, index - count).astype(jnp.float32)


def screened(wave_x, wave_y, wave_z):
    squared = (
        wave_x[:, None, None] * wave_x[:, None, None]
        + wave_y[None, :, None] * wave_y[None, :, None]
        + wave_z[None, None, :] * wave_z[None, None, :]
    )
    factor = NG / (2.0 * math.pi) * (NG / (2.0 * math.pi))
    return jnp.where(squared > 0.5, factor / (squared + SCREEN), jnp.float32(0.0))


def mult(data, table, form):
    return jnp.einsum(form, data, table, preferred_element_type=jnp.float32)


LANES = 128


def exchange_kernel(axes, total, gather, x_ref, o_ref, held, send_sem, recv_sem, own_sem):
    if len(axes) == 2:
        vec_count = lax.axis_size("vec")
        count = lax.axis_size("grid") * vec_count
        me = lax.axis_index("grid") * vec_count + lax.axis_index("vec")
    else:
        count = lax.axis_size(axes[0])
        me = lax.axis_index(axes[0])
    land = held if total else o_ref

    def place(index):
        if len(axes) == 2:
            return (index // vec_count, lax.rem(index, vec_count))
        if axes[0] == "grid":
            return (index, lax.axis_index("vec"))
        return (lax.axis_index("grid"), index)

    def part(index):
        return x_ref if gather else x_ref.at[index]

    barrier = pltpu.get_barrier_semaphore()

    def greet(step, carry):
        pl.semaphore_signal(
            barrier,
            inc=1,
            device_id=place(lax.rem(me + step, count)),
            device_id_type=pl.DeviceIdType.MESH,
        )
        return carry

    lax.fori_loop(1, count, greet, 0)
    own = pltpu.make_async_copy(part(me), land.at[me], own_sem)
    own.start()
    pl.semaphore_wait(barrier, count - 1)

    def copy(step, source, slot):
        peer = lax.rem(me + step, count)
        return pltpu.make_async_remote_copy(
            src_ref=part(source),
            dst_ref=land.at[slot],
            send_sem=send_sem.at[step],
            recv_sem=recv_sem.at[step],
            device_id=place(peer),
            device_id_type=pl.DeviceIdType.MESH,
        )

    def send(step, carry):
        copy(step, lax.rem(me + step, count), me).start()
        return carry

    lax.fori_loop(1, count, send, 0)
    own.wait()

    def receive(step, carry):
        source = lax.rem(me + count - step, count)
        copy(step, source, source).wait_recv()
        return carry

    lax.fori_loop(1, count, receive, 0)
    if total:
        o_ref[...] = jnp.sum(held[...].astype(jnp.float32), axis=0).astype(o_ref.dtype)

    def drain(step, carry):
        copy(step, lax.rem(me + step, count), me).wait_send()
        return carry

    lax.fori_loop(1, count, drain, 0)


def exchange(blocks, ident, total=False, axes=("grid", "vec"), gather=False):
    rows, lanes = blocks.shape[-2:]
    count = 1
    for axis in axes:
        count *= lax.axis_size(axis)
    shape = (rows, lanes) if total else (count, rows, lanes)
    held_shape = blocks.shape if total else (1, 8, LANES)

    def body(*refs):
        exchange_kernel(axes, total, gather, *refs)

    return pl.pallas_call(
        body,
        out_shape=jax.ShapeDtypeStruct(shape, blocks.dtype),
        in_specs=[pl.BlockSpec(memory_space=pltpu.VMEM)],
        out_specs=pl.BlockSpec(memory_space=pltpu.VMEM),
        scratch_shapes=[
            pltpu.VMEM(held_shape, blocks.dtype),
            pltpu.SemaphoreType.DMA((count,)),
            pltpu.SemaphoreType.DMA((count,)),
            pltpu.SemaphoreType.DMA(()),
        ],
        compiler_params=pltpu.CompilerParams(
            collective_id=ident, has_side_effects=True, vmem_limit_bytes=32 << 20
        ),
        name="exchange_total" if total else "exchange_gather" if gather else "exchange_blocks",
    )(blocks)


def share_rows(picked, grid_count, vec_count):
    npoints, norb = picked.shape
    if npoints % (grid_count * vec_count * 16) != 0:
        return lax.psum(picked.astype(jnp.float32), ("grid", "vec")).astype(picked.dtype)
    mine = exchange(
        picked.reshape(vec_count, npoints // vec_count, norb), 4, total=True, axes=("vec",)
    )
    mine = exchange(
        mine.reshape(grid_count, npoints // vec_count // grid_count, norb),
        5,
        total=True,
        axes=("grid",),
    )
    block = exchange(mine, 6, axes=("grid",), gather=True).reshape(npoints // vec_count, norb)
    return exchange(block, 7, axes=("vec",), gather=True).reshape(npoints, norb)


def transform(re, im, cos_tab, sin_tab, form, sign):
    out_re = mult(re, cos_tab, form) + sign * mult(im, sin_tab, form)
    out_im = mult(im, cos_tab, form) - sign * mult(re, sin_tab, form)
    return out_re, out_im


def solve_columns(fit_cols):
    bf = jnp.bfloat16
    count = fit_cols.shape[0]
    rows = fit_cols.shape[1]
    flat = exchange(fit_cols.reshape(count, rows // LANES, LANES), 1)
    field = flat.reshape(1, NG, NG, NG)
    cos_tab, sin_tab = wave_tables(NG)
    waves = wavenumber(lax.iota(jnp.int32, NG), NG)
    kernel = screened(waves, waves, waves)[None]
    a_re = mult(field, cos_tab, "vxyz,zk->vxyk").astype(bf)
    a_im = (-mult(field, sin_tab, "vxyz,zk->vxyk")).astype(bf)
    b_re, b_im = transform(a_re, a_im, cos_tab, sin_tab, "vxyz,yk->vxkz", 1.0)
    b_re, b_im = b_re.astype(bf), b_im.astype(bf)
    h_re, h_im = transform(b_re, b_im, cos_tab, sin_tab, "vxyz,xk->vkyz", 1.0)
    q_re, q_im = (h_re * kernel).astype(bf), (h_im * kernel).astype(bf)
    g_re, g_im = transform(q_re, q_im, cos_tab, sin_tab, "vxyz,xk->vkyz", -1.0)
    g_re, g_im = g_re.astype(bf), g_im.astype(bf)
    p_re, p_im = transform(g_re, g_im, cos_tab, sin_tab, "vxyz,yk->vxkz", -1.0)
    p_re, p_im = p_re.astype(bf), p_im.astype(bf)
    final = mult(p_re, cos_tab, "vxyz,zk->vxyk") - mult(p_im, sin_tab, "vxyz,zk->vxyk")
    potential = (final / float(NG**3)).astype(bf).reshape(flat.shape)
    return exchange(potential, 2).reshape(count, rows)


def project(pair, pot_rows):
    scale = 1.0 / math.sqrt(float(NG**3))
    term = lax.dot_general(
        pair, pot_rows, (((0,), (1,)), ((), ())), preferred_element_type=jnp.float32
    )
    term = term * jnp.float32(scale)
    npoints, cols = term.shape
    count = lax.axis_size("grid") * lax.axis_size("vec")
    share = npoints // count
    if share * cols % LANES == 0:
        blocks = term.reshape(count, share * cols // LANES, LANES)
        return exchange(blocks, 3, True).reshape(share, cols)
    partial_block = lax.psum_scatter(term, "grid", scatter_dimension=0, tiled=True)
    return lax.psum_scatter(partial_block, "vec", scatter_dimension=0, tiled=True)


def shards(orbitals, inverse_panel, points):
    bf = jnp.bfloat16
    row_count = orbitals.shape[0]
    grid_count = lax.axis_size("grid")
    vec_count = lax.axis_size("vec")
    npoints = points.shape[0]
    offset = (lax.axis_index("grid") * vec_count + lax.axis_index("vec")) * row_count
    local_pos = points - offset
    inside = (local_pos >= 0) & (local_pos < row_count)
    picked = jnp.take(orbitals, jnp.clip(local_pos, 0, row_count - 1), axis=0)
    picked = jnp.where(inside[:, None], picked, jnp.zeros_like(picked))
    point_rows = share_rows(picked, grid_count, vec_count)

    def pair_block(block):
        correlation = lax.dot_general(
            block, point_rows, (((1,), (1,)), ((), ())), preferred_element_type=jnp.float32
        )
        return (correlation * correlation).astype(bf)

    pair = lax.map(pair_block, orbitals.reshape(4, row_count // 4, orbitals.shape[1])).reshape(
        row_count, npoints
    )
    fit_cols = lax.dot_general(
        inverse_panel, pair, (((0,), (1,)), ((), ())), preferred_element_type=jnp.float32
    ).astype(bf)
    if inverse_panel.shape[1] == grid_count * vec_count and row_count % LANES == 0:
        return project(pair, solve_columns(fit_cols))
    slab = lax.all_to_all(fit_cols, "vec", split_axis=0, concat_axis=1, tiled=True)
    col_local = slab.shape[0]
    planes = NG // grid_count
    field = slab.reshape(col_local, planes, NG, NG)
    cos_tab, sin_tab = wave_tables(NG)
    z_re = mult(field, cos_tab, "vxyz,zk->vxyk").astype(bf)
    z_im = (-mult(field, sin_tab, "vxyz,zk->vxyk")).astype(bf)
    y_re = (mult(z_re, cos_tab, "vxyz,yk->vxkz") + mult(z_im, sin_tab, "vxyz,yk->vxkz")).astype(bf)
    y_im = (mult(z_im, cos_tab, "vxyz,yk->vxkz") - mult(z_re, sin_tab, "vxyz,yk->vxkz")).astype(bf)
    stacked = jnp.stack([y_re, y_im])
    waves = wavenumber(lax.iota(jnp.int32, NG), NG)
    y_waves = wavenumber(lax.axis_index("grid") * planes + lax.iota(jnp.int32, planes), NG)
    kernel = screened(waves, y_waves, waves)[None]
    piece = lax.all_to_all(stacked, "grid", split_axis=3, concat_axis=2, tiled=True)
    p_re = piece[0]
    p_im = piece[1]
    x_re = mult(p_re, cos_tab, "vxyz,xk->vkyz") + mult(p_im, sin_tab, "vxyz,xk->vkyz")
    x_im = mult(p_im, cos_tab, "vxyz,xk->vkyz") - mult(p_re, sin_tab, "vxyz,xk->vkyz")
    q_re = (x_re * kernel).astype(bf)
    q_im = (x_im * kernel).astype(bf)
    i_re = (mult(q_re, cos_tab, "vxyz,xk->vkyz") - mult(q_im, sin_tab, "vxyz,xk->vkyz")).astype(bf)
    i_im = (mult(q_im, cos_tab, "vxyz,xk->vkyz") + mult(q_re, sin_tab, "vxyz,xk->vkyz")).astype(bf)
    spectrum = lax.all_to_all(
        jnp.stack([i_re, i_im]), "grid", split_axis=2, concat_axis=3, tiled=True
    )
    s_re = spectrum[0]
    s_im = spectrum[1]
    h_re = (mult(s_re, cos_tab, "vxyz,yk->vxkz") - mult(s_im, sin_tab, "vxyz,yk->vxkz")).astype(bf)
    h_im = (mult(s_im, cos_tab, "vxyz,yk->vxkz") + mult(s_re, sin_tab, "vxyz,yk->vxkz")).astype(bf)
    final = mult(h_re, cos_tab, "vxyz,zk->vxyk") - mult(h_im, sin_tab, "vxyz,zk->vxyk")
    potential = (final / float(NG**3)).astype(bf).reshape(col_local, planes * NG * NG)
    pot_rows = lax.all_to_all(potential, "vec", split_axis=1, concat_axis=0, tiled=True)
    return project(pair, pot_rows)


def solution(mesh):
    in_specs = (P(("grid", "vec"), None), P(), P())
    out_specs = P(("grid", "vec"), None)
    return jax.shard_map(shards, mesh=mesh, in_specs=in_specs, out_specs=out_specs, check_vma=False)
```
